32 devices in a mesh: grp: 4 (over z), leaf: 8 (over y, x, core).
Axes of the slice: x: 2, y: 2, z: 4, core: 2. Of those that a mesh axis runs over, the one named last changes fastest.
Arguments:
- basis_slab: bfloat16 [32768, 1024], P(('grp', 'leaf')), may hold values from -6 to 6
- live_counts: int32 [32], P(('grp', 'leaf')), may hold values from 128 to 1024, as said below
- pole_order: int32 [32, 1024], P(('grp', 'leaf')), may hold values from 0 to 1023, each once within a row
- leaf_diag: bfloat16 [32768, 1024], P(('grp', 'leaf')), may hold values from -0.1875 to 0.1875
- leaf_in: bfloat16 [32768, 128], P(('grp', 'leaf')), may hold values from -0.1875 to 0.1875
- leaf_out: bfloat16 [32768, 128], P(('grp', 'leaf')), may hold values from -0.5 to 0.5
- leaf_lift: bfloat16 [32, 128, 128], P(('grp', 'leaf')), may hold values from -0.375 to 0.375
- leaf_couple: bfloat16 [32, 128, 128], P(('grp', 'leaf')), may hold values from -0.5 to 0.5
- leaf_spread: bfloat16 [32, 128, 128], P(('grp', 'leaf')), may hold values from -0.4375 to 0.4375
- inner_lift: bfloat16 [28, 128, 128], replicated, may hold values from -0.375 to 0.375
- inner_couple: bfloat16 [30, 128, 128], replicated, may hold values from -0.5 to 0.5
- inner_spread: bfloat16 [28, 128, 128], replicated, may hold values from -0.4375 to 0.4375
Outputs:
- merged: bfloat16 [32768, 1024], P(('grp', 'leaf'))
The draws below stay inside these ranges and needn't reach their ends.
Inputs may be any that keep to these rules, and one draw needn't show every extreme that they name: `live_counts`: each count is 1024, 512, 256 or 128, and some leaf has 1024. `pole_order`: each row names every slot's pole once.
All inputs are finite; a program needn't handle non-finite values.
Results may differ from the reference program's by a relative error of at most 0.0055.
Values may be sent and summed in bfloat16 or wider, within the bound.
A program may use at most 64 MiB of HBM per device.

```python
import jax
import jax.numpy as jnp
from jax import lax

M = 1024
RANK = 128
R = 1024
N = 32768
N_GRP = 4
N_LEAF = 8
DEVICES = 32


def draw_live_counts(key, part):
    first_key, second_key = jax.random.split(jax.random.fold_in(key, 17))
    halvings = jax.random.randint(first_key, (N_GRP * N_LEAF,), 0, 4)
    counts = jnp.right_shift(jnp.full((N_GRP * N_LEAF,), M, jnp.int32), halvings.astype(jnp.int32))
    fullest = jax.random.randint(second_key, (), 0, N_GRP * N_LEAF)
    return counts.at[fullest].set(M).astype(jnp.int32)


def block_scale(key, dims, cuts, low, largest):
    gain = 1.0
    for axis_at, parts in cuts:
        draws = jax.random.uniform(jax.random.fold_in(jax.random.fold_in(key, 6), axis_at), (parts,), jnp.float32, low / len(cuts), largest / len(cuts))
        gain = gain * jnp.repeat(jnp.exp(draws), dims[axis_at] // parts).reshape((-1,) + (1,) * (len(dims) - 1 - axis_at))
    return gain


def scatter_about(key, extent, spread, limit, cuts=(), kind=jnp.bfloat16):
    drawn = spread * jax.random.normal(key, extent, jnp.float32)
    if cuts:
        drawn = drawn * block_scale(key, extent, cuts, -0.22, 0.18)
    return jnp.clip(drawn, -limit, limit).astype(kind)


def setup_inputs(seed: int = 0) -> dict:
    seeds = jax.random.split(jax.random.key(seed), 13)
    return {
        "basis_slab": scatter_about(seeds[0], (N, R), 1.0, 6.0, ((0, 32),)),
        "live_counts": draw_live_counts(jax.random.fold_in(seeds[12], 71), 0),
        "pole_order": jax.vmap(lambda own: jax.random.permutation(own, M))(jax.random.split(seeds[2], DEVICES)).reshape((DEVICES, M)).astype(jnp.int32),
        "leaf_diag": scatter_about(seeds[3], (N, M), M ** -0.5, 0.1875, ((0, 32),)),
        "leaf_in": scatter_about(seeds[4], (N, RANK), M ** -0.5, 0.1875, ((0, 32),)),
        "leaf_out": scatter_about(seeds[5], (N, RANK), RANK ** -0.5, 0.5, ((0, 32),)),
        "leaf_lift": scatter_about(seeds[6], (DEVICES, RANK, RANK), (2 * RANK) ** -0.5, 0.375, ((0, 32),)),
        "leaf_couple": scatter_about(seeds[7], (DEVICES, RANK, RANK), RANK ** -0.5, 0.5, ((0, 32),)),
        "leaf_spread": scatter_about(seeds[8], (DEVICES, RANK, RANK), (3 * RANK // 2) ** -0.5, 0.4375, ((0, 32),)),
        "inner_lift": scatter_about(seeds[9], (DEVICES - 4, RANK, RANK), (2 * RANK) ** -0.5, 0.375),
        "inner_couple": scatter_about(seeds[10], (DEVICES - 2, RANK, RANK), RANK ** -0.5, 0.5),
        "inner_spread": scatter_about(seeds[11], (DEVICES - 4, RANK, RANK), (3 * RANK // 2) ** -0.5, 0.4375),
    }


def full_product(matrices, stacked):
    return jnp.einsum('nij,njc->nic', matrices.astype(jnp.float32), stacked, precision=lax.Precision.HIGHEST)


def leaf_skeleton(pieces):
    generator, masked = pieces
    return jnp.einsum('mk,mc->kc', generator, masked, preferred_element_type=jnp.float32)


def leaf_update(pieces):
    diagonal, generator, masked, incoming = pieces
    return jnp.dot(diagonal, masked, preferred_element_type=jnp.float32) + jnp.dot(generator, incoming, preferred_element_type=jnp.float32)


def reference(basis_slab, live_counts, pole_order, leaf_diag, leaf_in, leaf_out, leaf_lift, leaf_couple, leaf_spread, inner_lift, inner_couple, inner_spread):
    devices = N_GRP * N_LEAF
    block_rows = M // devices
    levels = devices.bit_length() - 1
    leaf_rows = basis_slab.reshape(devices, devices, block_rows, R).transpose(1, 0, 2, 3).reshape(devices, M, R)
    slots = jnp.take_along_axis(leaf_rows, pole_order.astype(jnp.int32)[:, :, None], axis=1)
    live_mask = jnp.arange(M, dtype=jnp.int32)[None, :] < live_counts[:, None]
    masked = jnp.where(live_mask[:, :, None], slots, jnp.zeros_like(slots))
    skeleton = lax.map(leaf_skeleton, (leaf_in.reshape(devices, M, RANK), masked))
    crosses = []
    for height in range(levels):
        node_count = devices >> height
        couples = leaf_couple if height == 0 else inner_couple[node_count - 2:2 * node_count - 2]
        coupled = full_product(couples, skeleton)
        crosses.append(coupled.reshape(node_count // 2, 2, RANK, R)[:, ::-1].reshape(node_count, RANK, R))
        if height < levels - 1:
            lifts = leaf_lift if height == 0 else inner_lift[node_count - 4:2 * node_count - 4]
            lifted = full_product(lifts, skeleton)
            skeleton = lifted[0::2] + lifted[1::2]
    incoming = crosses[levels - 1]
    for height in range(levels - 2, -1, -1):
        node_count = devices >> height
        spreads = leaf_spread if height == 0 else inner_spread[node_count - 4:2 * node_count - 4]
        parent = jnp.repeat(incoming, 2, axis=0)
        incoming = full_product(spreads, parent) + crosses[height]
    incoming_b = incoming.astype(jnp.bfloat16)
    updated = lax.map(leaf_update, (leaf_diag.reshape(devices, M, M), leaf_out.reshape(devices, M, RANK), masked, incoming_b))
    updated = jnp.where(live_mask[:, :, None], updated, slots.astype(jnp.float32)).astype(jnp.bfloat16)
    inverse = jnp.zeros((devices, M), jnp.int32).at[jnp.arange(devices, dtype=jnp.int32)[:, None], pole_order.astype(jnp.int32)].set(jnp.broadcast_to(jnp.arange(M, dtype=jnp.int32), (devices, M)))
    restored = jnp.take_along_axis(updated, inverse[:, :, None], axis=1)
    return restored.reshape(devices, devices, block_rows, R).transpose(1, 0, 2, 3).reshape(N, R)
```

```python
import functools

import jax
import jax.numpy as jnp
from jax import lax
from jax.experimental import pallas as pl
from jax.experimental.pallas import tpu as pltpu
from jax.sharding import PartitionSpec as P

MESH = pl.DeviceIdType.MESH
CHUNKS = 4
AHEAD = 2
STRIDE = 3


def row_dot(a, b):
    return jnp.dot(a, b, preferred_element_type=jnp.float32)


def fine_dot(matrix, value):
    high = value.astype(jnp.bfloat16)
    low = (value - high.astype(jnp.float32)).astype(jnp.bfloat16)
    return row_dot(matrix, high) + row_dot(matrix, low)


def fused_kernel(
    groups,
    leaves,
    slab,
    live,
    order,
    diag,
    gen_in,
    gen_out,
    leaf_lift,
    leaf_couple,
    leaf_spread,
    inner_lift,
    inner_couple,
    inner_spread,
    out,
    arrived,
    staged,
    select,
    diag_poles,
    in_poles,
    out_poles,
    leaf_sent,
    leaf_got,
    sent,
    got,
    cross,
    own,
    in_send,
    in_recv,
    out_send,
    out_recv,
    tree_send,
    tree_recv,
    local_sem,
):
    devices = groups * leaves
    levels = devices.bit_length() - 1
    chunks, width, cols = arrived.shape
    block = width // devices
    me = lax.axis_index("grp") * leaves + lax.axis_index("leaf")

    def place(device):
        return (lax.div(device, leaves), lax.rem(device, leaves))

    def node(height):
        return lax.div(devices + me, 1 << height)

    def sibling(index):
        return index + 1 - 2 * lax.rem(index, 2)

    def partner(height):
        bit = lax.rem(lax.div(me, 1 << height), 2)
        return place(me + (1 - 2 * bit) * (1 << height))

    def others(step):
        def body(shift, carry):
            step(lax.rem(me + shift, devices))
            return carry

        lax.fori_loop(1, devices, body, 0)

    def rows_of(device):
        return pl.ds(pl.multiple_of(device * block, block), block)

    def cols_of(chunk):
        return pl.ds(chunk * cols, cols)

    barrier = pltpu.get_barrier_semaphore()
    others(
        lambda device: pl.semaphore_signal(
            barrier, inc=1, device_id=place(device), device_id_type=MESH
        )
    )
    pl.semaphore_wait(barrier, devices - 1)

    def send_in(chunk):
        others(
            lambda device: pltpu.make_async_remote_copy(
                src_ref=slab.at[rows_of(device), cols_of(chunk)],
                dst_ref=arrived.at[chunk, rows_of(me)],
                send_sem=in_send.at[chunk],
                recv_sem=in_recv.at[chunk],
                device_id=place(device),
                device_id_type=MESH,
            ).start()
        )
        pltpu.make_async_copy(
            slab.at[rows_of(me), cols_of(chunk)],
            arrived.at[chunk, rows_of(me)],
            local_sem.at[0, chunk],
        ).start()

    def send_out(chunk):
        others(
            lambda device: pltpu.make_async_remote_copy(
                src_ref=staged.at[chunk, rows_of(device)],
                dst_ref=out.at[rows_of(me), cols_of(chunk)],
                send_sem=out_send.at[chunk],
                recv_sem=out_recv.at[chunk],
                device_id=place(device),
                device_id_type=MESH,
            ).start()
        )
        pltpu.make_async_copy(
            staged.at[chunk, rows_of(me)],
            out.at[rows_of(me), cols_of(chunk)],
            local_sem.at[1, chunk],
        ).start()

    def wait_all(buffer, semaphore):
        most = buffer.at[pl.ds(0, width - block)]
        pltpu.make_async_copy(most, most, semaphore).wait()

    def wait_own(buffer, semaphore):
        part = buffer.at[pl.ds(0, block)]
        pltpu.make_async_copy(part, part, semaphore).wait()

    def tree_copy(chunk, height):
        source, target = (
            (leaf_sent.at[chunk], leaf_got.at[chunk])
            if height == 0
            else (sent.at[chunk, height - 1], got.at[chunk, height - 1])
        )
        return pltpu.make_async_remote_copy(
            src_ref=source,
            dst_ref=target,
            send_sem=tree_send.at[chunk, height],
            recv_sem=tree_recv.at[chunk, height],
            device_id=partner(height),
            device_id_type=MESH,
        )

    for chunk in range(min(AHEAD, chunks)):
        send_in(chunk)

    slot = lax.broadcasted_iota(jnp.int32, (1, width), 1)
    key = jnp.where(slot < live[...], order[...], -1)
    part = min(256, width)
    for start in range(0, width, part):
        pole = lax.broadcasted_iota(jnp.int32, (part, width), 0) + start
        select[start : start + part, :] = jnp.where(pole == key, 1.0, 0.0).astype(jnp.bfloat16)

    def fold(index, carry):
        start = pl.multiple_of(index * part, part)
        rows = pl.ds(start, part)
        chosen = select[rows, :]
        half = row_dot(chosen, diag[...]).astype(jnp.bfloat16)
        full = lax.dot_general(
            half, select[...], (((1,), (1,)), ((), ())), preferred_element_type=jnp.float32
        )
        alive = jnp.sum(chosen.astype(jnp.float32), axis=1, keepdims=True)
        pole = lax.broadcasted_iota(jnp.int32, (part, width), 0) + start
        same = jnp.where(pole == lax.broadcasted_iota(jnp.int32, (part, width), 1), 1.0, 0.0)
        diag_poles[rows, :] = (full + (1.0 - alive) * same).astype(jnp.bfloat16)
        out_poles[rows, :] = row_dot(chosen, gen_out[...]).astype(jnp.bfloat16)
        in_poles[rows, :] = row_dot(chosen, gen_in[...])
        return carry

    lax.fori_loop(0, width // part, fold, 0)
    gather = in_poles[...].T.astype(jnp.bfloat16)

    def first(chunk):
        wait_all(arrived.at[chunk], in_recv.at[chunk])
        wait_own(arrived.at[chunk], local_sem.at[0, chunk])
        skeleton = row_dot(gather, arrived[chunk])
        lifted = fine_dot(leaf_lift[0], skeleton)
        own[chunk] = lifted
        leaf_sent[chunk, 0] = lifted.astype(jnp.bfloat16)
        leaf_sent[chunk, 1] = fine_dot(leaf_couple[0], skeleton).astype(jnp.bfloat16)
        tree_copy(chunk, 0).start()

    def rise(chunk, height):
        tree_copy(chunk, height).wait()
        if height == 0:
            cross[chunk, 0] = leaf_got[chunk, 1].astype(jnp.float32)
            skeleton = own[chunk] + leaf_got[chunk, 0].astype(jnp.float32)
        else:
            mine = node(height)
            other = sibling(mine)
            theirs = got[chunk, height - 1]
            cross[chunk, height] = row_dot(inner_couple[other - 2], theirs)
            if height == levels - 1:
                return
            skeleton = fine_dot(inner_lift[mine - 4], own[chunk]) + row_dot(
                inner_lift[other - 4], theirs
            )
        own[chunk] = skeleton
        sent[chunk, height] = skeleton.astype(jnp.bfloat16)
        tree_copy(chunk, height + 1).start()

    def finish(chunk):
        incoming = cross[chunk, levels - 1]
        for height in range(levels - 2, -1, -1):
            spread = leaf_spread[0] if height == 0 else inner_spread[node(height) - 4]
            incoming = fine_dot(spread, incoming) + cross[chunk, height]
        incoming = incoming.astype(jnp.bfloat16)

        def rows_done(index, carry):
            rows = pl.ds(pl.multiple_of(index * part, part), part)
            value = row_dot(diag_poles[rows, :], arrived[chunk]) + row_dot(
                out_poles[rows, :], incoming
            )
            staged[chunk, rows, :] = value.astype(jnp.bfloat16)
            return carry

        lax.fori_loop(0, width // part, rows_done, 0)
        send_out(chunk)

    for tick in range(STRIDE * (chunks - 1) + levels + 1):
        for chunk in range(chunks):
            stage = tick - STRIDE * chunk
            if stage == 0:
                first(chunk)
                if chunk + AHEAD < chunks:
                    send_in(chunk + AHEAD)
            elif 1 <= stage <= levels:
                rise(chunk, stage - 1)
                if stage == levels:
                    finish(chunk)

    for chunk in range(chunks):
        wait_all(arrived.at[chunk], in_send.at[chunk])
        wait_all(staged.at[chunk], out_send.at[chunk])
        wait_all(staged.at[chunk], out_recv.at[chunk])
        wait_own(staged.at[chunk], local_sem.at[1, chunk])


def fused(
    basis_slab,
    live_counts,
    pole_order,
    leaf_diag,
    leaf_in,
    leaf_out,
    leaf_lift,
    leaf_couple,
    leaf_spread,
    inner_lift,
    inner_couple,
    inner_spread,
):
    groups = lax.axis_size("grp")
    leaves = lax.axis_size("leaf")
    devices = groups * leaves
    levels = devices.bit_length() - 1
    width, slab_rows = basis_slab.shape
    rank = leaf_in.shape[1]
    cols = slab_rows // CHUNKS
    vmem = pl.BlockSpec(memory_space=pltpu.VMEM)
    anywhere = pl.BlockSpec(memory_space=pl.ANY)
    half = jnp.bfloat16
    return pl.pallas_call(
        functools.partial(fused_kernel, groups, leaves),
        out_shape=jax.ShapeDtypeStruct((width, slab_rows), half),
        in_specs=[anywhere] + [vmem] * 11,
        out_specs=anywhere,
        scratch_shapes=[
            pltpu.VMEM((CHUNKS, width, cols), half),
            pltpu.VMEM((CHUNKS, width, cols), half),
            pltpu.VMEM((width, width), half),
            pltpu.VMEM((width, width), half),
            pltpu.VMEM((width, rank), jnp.float32),
            pltpu.VMEM((width, rank), half),
            pltpu.VMEM((CHUNKS, 2, rank, cols), half),
            pltpu.VMEM((CHUNKS, 2, rank, cols), half),
            pltpu.VMEM((CHUNKS, levels - 1, rank, cols), half),
            pltpu.VMEM((CHUNKS, levels - 1, rank, cols), half),
            pltpu.VMEM((CHUNKS, levels, rank, cols), jnp.float32),
            pltpu.VMEM((CHUNKS, rank, cols), jnp.float32),
            pltpu.SemaphoreType.DMA((CHUNKS,)),
            pltpu.SemaphoreType.DMA((CHUNKS,)),
            pltpu.SemaphoreType.DMA((CHUNKS,)),
            pltpu.SemaphoreType.DMA((CHUNKS,)),
            pltpu.SemaphoreType.DMA((CHUNKS, levels)),
            pltpu.SemaphoreType.DMA((CHUNKS, levels)),
            pltpu.SemaphoreType.DMA((2, CHUNKS)),
        ],
        compiler_params=pltpu.CompilerParams(
            collective_id=0, has_side_effects=True, vmem_limit_bytes=56 * 1024 * 1024
        ),
    )(
        basis_slab,
        live_counts.reshape(1, 1),
        pole_order,
        leaf_diag,
        leaf_in,
        leaf_out,
        leaf_lift,
        leaf_couple,
        leaf_spread,
        inner_lift,
        inner_couple,
        inner_spread,
    )


def from_partner(block, axis, apart):
    count = lax.axis_size(axis)
    route = []
    for low in range(count):
        high = low | 1 << apart
        if high != low and high < count:
            route += [(low, high), (high, low)]
    return lax.ppermute(block, axis, route)


def transform(matrix, stacked):
    return jnp.dot(matrix.astype(jnp.float32), stacked, precision=lax.Precision.HIGHEST)


def local(
    basis_slab,
    live_counts,
    pole_order,
    leaf_diag,
    leaf_in,
    leaf_out,
    leaf_lift,
    leaf_couple,
    leaf_spread,
    inner_lift,
    inner_couple,
    inner_spread,
):
    groups = lax.axis_size("grp")
    leaves = lax.axis_size("leaf")
    devices = groups * leaves
    leaf_width = basis_slab.shape[0]
    slab_rows = basis_slab.shape[1]
    block_rows = leaf_width // devices
    levels = devices.bit_length() - 1
    leaf_bits = leaves.bit_length() - 1
    position = lax.axis_index("grp") * leaves + lax.axis_index("leaf")

    def redistribute(columns):
        arrived = lax.all_to_all(
            columns.reshape(devices, block_rows, slab_rows),
            ("grp", "leaf"),
            split_axis=0,
            concat_axis=0,
            tiled=True,
        )
        return arrived.reshape(leaf_width, slab_rows)

    def node_matrix(height, leaf_table, inner_table, offset):
        if height == 0:
            return leaf_table[0]
        own_node = jnp.right_shift(devices + position, height)
        return lax.dynamic_index_in_dim(inner_table, own_node - offset, 0, keepdims=False)

    leaf_rows = redistribute(basis_slab)
    slot_order = pole_order[0]
    live_count = live_counts[0]
    slots = jnp.take(leaf_rows, slot_order, axis=0)
    live_mask = jnp.arange(leaf_width, dtype=jnp.int32) < live_count
    masked = jnp.where(live_mask[:, None], slots, jnp.zeros_like(slots))
    skeleton = jnp.einsum("mk,mc->kc", leaf_in, masked, preferred_element_type=jnp.float32)
    crosses = []
    for height in range(leaf_bits):
        lifted = transform(node_matrix(height, leaf_lift, inner_lift, 4), skeleton)
        coupled = transform(node_matrix(height, leaf_couple, inner_couple, 2), skeleton)
        other_lift, other_cross = from_partner((lifted, coupled), "leaf", height)
        crosses.append(other_cross)
        skeleton = lifted + other_lift
    group_bits = groups.bit_length() - 1
    for height in range(leaf_bits, levels - 1):
        lifted = transform(node_matrix(height, leaf_lift, inner_lift, 4), skeleton)
        coupled = transform(node_matrix(height, leaf_couple, inner_couple, 2), skeleton)
        other_lift, other_cross = (
            from_partner(lifted.astype(jnp.bfloat16), "grp", height - leaf_bits).astype(
                lifted.dtype
            ),
            from_partner(coupled.astype(jnp.bfloat16), "grp", height - leaf_bits).astype(
                coupled.dtype
            ),
        )
        crosses.append(other_cross)
        skeleton = lifted + other_lift
    coupled = transform(node_matrix(levels - 1, leaf_couple, inner_couple, 2), skeleton)
    crosses.append(
        from_partner(coupled.astype(jnp.bfloat16), "grp", group_bits - 1).astype(coupled.dtype)
    )
    incoming = crosses[levels - 1]
    for height in range(levels - 2, -1, -1):
        incoming = (
            transform(node_matrix(height, leaf_spread, inner_spread, 4), incoming) + crosses[height]
        )
    incoming_b = incoming.astype(jnp.bfloat16)
    tile_rows = leaf_width // 8
    tile_count = live_count // tile_rows

    def one_tile(tile_index, merged_rows):
        row_start = tile_index * tile_rows
        diag_rows = lax.dynamic_slice_in_dim(leaf_diag, row_start, tile_rows, 0)
        out_rows = lax.dynamic_slice_in_dim(leaf_out, row_start, tile_rows, 0)
        value = jnp.dot(diag_rows, masked, preferred_element_type=jnp.float32) + jnp.dot(
            out_rows, incoming_b, preferred_element_type=jnp.float32
        )
        return lax.dynamic_update_slice_in_dim(merged_rows, value, row_start, 0)

    merged_rows = lax.fori_loop(
        0, tile_count, one_tile, jnp.zeros((leaf_width, slab_rows), jnp.float32)
    )
    updated = jnp.where(live_mask[:, None], merged_rows, slots.astype(jnp.float32)).astype(
        jnp.bfloat16
    )
    inverse = (
        jnp.zeros((leaf_width,), jnp.int32)
        .at[slot_order]
        .set(jnp.arange(leaf_width, dtype=jnp.int32))
    )
    restored = jnp.take(updated, inverse, axis=0)
    return redistribute(restored)


def solution(mesh):
    placed = (
        P(("grp", "leaf"), None),
        P(("grp", "leaf")),
        P(("grp", "leaf"), None),
        P(("grp", "leaf"), None),
        P(("grp", "leaf"), None),
        P(("grp", "leaf"), None),
        P(("grp", "leaf"), None, None),
        P(("grp", "leaf"), None, None),
        P(("grp", "leaf"), None, None),
        P(),
        P(),
        P(),
    )

    def step(basis_slab, *rest):
        devices = mesh.shape["grp"] * mesh.shape["leaf"]
        block_rows = basis_slab.shape[0] // devices
        whole_tiles = block_rows % 16 == 0 and basis_slab.shape[1] % (128 * CHUNKS) == 0
        return (fused if whole_tiles else local)(basis_slab, *rest)

    return jax.shard_map(
        step, mesh=mesh, in_specs=placed, out_specs=P(("grp", "leaf"), None), check_vma=False
    )
```

```python
import functools

import jax
import jax.numpy as jnp
from jax import lax
from jax.experimental import pallas as pl
from jax.experimental.pallas import tpu as pltpu
from jax.sharding import PartitionSpec as P

MESH = pl.DeviceIdType.MESH
CHUNKS = 4
AHEAD = 2
STRIDE = 1


def row_dot(a, b):
    return jnp.dot(a, b, preferred_element_type=jnp.float32)


def times(matrix, rows):
    return lax.dot_general(
        rows, matrix, (((1,), (1,)), ((), ())), preferred_element_type=jnp.float32
    )


def fine_times(matrix, rows):
    high = rows.astype(jnp.bfloat16)
    low = (rows - high.astype(jnp.float32)).astype(jnp.bfloat16)
    return times(matrix, high) + times(matrix, low)


def fused_kernel(
    groups,
    leaves,
    slab,
    live,
    order,
    diag,
    gen_in,
    gen_out,
    leaf_lift,
    leaf_couple,
    leaf_spread,
    inner_lift,
    inner_couple,
    inner_spread,
    out,
    arrived,
    staged,
    diag_here,
    in_here,
    out_here,
    lifts,
    couples,
    spreads,
    leaf_tables,
    select,
    diag_poles,
    in_poles,
    out_poles,
    up_sent,
    up_got,
    top,
    cross,
    down_sent,
    down_got,
    in_send,
    in_recv,
    out_send,
    out_recv,
    tree_send,
    tree_recv,
    local_sem,
    load_sem,
    table_send,
    table_recv,
):
    devices = groups * leaves
    chunks, width, cols = arrived.shape
    block = width // devices
    part_cols = cols // leaves
    group = lax.axis_index("grp")
    seat = lax.axis_index("leaf")
    me = group * leaves + seat

    def place(device):
        return (lax.div(device, leaves), lax.rem(device, leaves))

    def node(height):
        return lax.div(devices + me, 1 << height)

    def sibling(index):
        return index + 1 - 2 * lax.rem(index, 2)

    def seats(step):
        def body(shift, carry):
            step(lax.rem(seat + shift, leaves))
            return carry

        lax.fori_loop(1, leaves, body, 0)

    def others(step):
        def body(shift, carry):
            step(lax.rem(me + shift, devices))
            return carry

        lax.fori_loop(1, devices, body, 0)

    def rows_of(device):
        return pl.ds(pl.multiple_of(device * block, block), block)

    def cols_of(chunk):
        return pl.ds(chunk * cols, cols)

    barrier = pltpu.get_barrier_semaphore()
    others(
        lambda device: pl.semaphore_signal(
            barrier, inc=1, device_id=place(device), device_id_type=MESH
        )
    )
    pl.semaphore_wait(barrier, devices - 1)

    def send_in(chunk):
        others(
            lambda device: pltpu.make_async_remote_copy(
                src_ref=slab.at[rows_of(device), cols_of(chunk)],
                dst_ref=arrived.at[chunk, rows_of(me)],
                send_sem=in_send.at[chunk],
                recv_sem=in_recv.at[chunk],
                device_id=place(device),
                device_id_type=MESH,
            ).start()
        )
        pltpu.make_async_copy(
            slab.at[rows_of(me), cols_of(chunk)],
            arrived.at[chunk, rows_of(me)],
            local_sem.at[0, chunk],
        ).start()

    def send_out(chunk):
        others(
            lambda device: pltpu.make_async_remote_copy(
                src_ref=staged.at[chunk, rows_of(device)],
                dst_ref=out.at[rows_of(me), cols_of(chunk)],
                send_sem=out_send.at[chunk],
                recv_sem=out_recv.at[chunk],
                device_id=place(device),
                device_id_type=MESH,
            ).start()
        )
        pltpu.make_async_copy(
            staged.at[chunk, rows_of(me)],
            out.at[rows_of(me), cols_of(chunk)],
            local_sem.at[1, chunk],
        ).start()

    def wait_all(buffer, semaphore):
        most = buffer.at[pl.ds(0, width - block)]
        pltpu.make_async_copy(most, most, semaphore).wait()

    def wait_own(buffer, semaphore):
        part = buffer.at[pl.ds(0, block)]
        pltpu.make_async_copy(part, part, semaphore).wait()

    def tree_copy(source, target, chunk, stage, device):
        return pltpu.make_async_remote_copy(
            src_ref=source,
            dst_ref=target,
            send_sem=tree_send.at[stage, chunk],
            recv_sem=tree_recv.at[stage, chunk],
            device_id=device,
            device_id_type=MESH,
        )

    own_tables = (leaf_lift, leaf_couple, leaf_spread)
    for index, table in enumerate(own_tables):
        seats(
            lambda other: pltpu.make_async_remote_copy(
                src_ref=table.at[0],
                dst_ref=leaf_tables.at[seat, index],
                send_sem=table_send.at[0],
                recv_sem=table_recv.at[0],
                device_id=(group, other),
                device_id_type=MESH,
            ).start()
        )

    for chunk in range(min(AHEAD, chunks)):
        send_in(chunk)

    pairs = [(diag, diag_here), (gen_in, in_here), (gen_out, out_here)]
    pairs += [(inner_lift, lifts), (inner_couple, couples), (inner_spread, spreads)]
    pairs += [(table.at[0], leaf_tables.at[seat, index]) for index, table in enumerate(own_tables)]
    loads = [
        pltpu.make_async_copy(source, target, load_sem.at[index])
        for index, (source, target) in enumerate(pairs)
    ]
    for load in loads:
        load.start()

    slot = lax.broadcasted_iota(jnp.int32, (1, width), 1)
    key = jnp.where(slot < live[...], order[...], -1)
    part = min(256, width)
    for start in range(0, width, part):
        pole = lax.broadcasted_iota(jnp.int32, (part, width), 0) + start
        select[start : start + part, :] = jnp.where(pole == key, 1.0, 0.0).astype(jnp.bfloat16)

    for load in loads:
        load.wait()

    def fold(index, carry):
        start = pl.multiple_of(index * part, part)
        rows = pl.ds(start, part)
        chosen = select[rows, :]
        half = row_dot(chosen, diag_here[...]).astype(jnp.bfloat16)
        full = lax.dot_general(
            half, select[...], (((1,), (1,)), ((), ())), preferred_element_type=jnp.float32
        )
        alive = jnp.sum(chosen.astype(jnp.float32), axis=1, keepdims=True)
        pole = lax.broadcasted_iota(jnp.int32, (part, width), 0) + start
        same = jnp.where(pole == lax.broadcasted_iota(jnp.int32, (part, width), 1), 1.0, 0.0)
        diag_poles[rows, :] = (full + (1.0 - alive) * same).astype(jnp.bfloat16)
        out_poles[rows, :] = row_dot(chosen, out_here[...]).astype(jnp.bfloat16)
        in_poles[rows, :] = row_dot(chosen, in_here[...])
        return carry

    lax.fori_loop(0, width // part, fold, 0)
    gather = in_poles[...].T.astype(jnp.bfloat16)

    few = leaf_tables.at[pl.ds(0, leaves - 1)]
    pltpu.make_async_copy(few, few, table_recv.at[0]).wait()

    def seat_rows(other):
        return pl.ds(pl.multiple_of(other * part_cols, part_cols), part_cols)

    def wait_up(chunk, semaphore):
        most = up_got.at[chunk, pl.ds(0, leaves - 1)]
        pltpu.make_async_copy(most, most, semaphore).wait()

    def wait_top(chunk, semaphore):
        most = top.at[chunk, pl.ds(0, groups - 1)]
        pltpu.make_async_copy(most, most, semaphore).wait()

    def wait_down(chunk, semaphore):
        most = down_got.at[chunk, pl.ds(0, cols - part_cols)]
        pltpu.make_async_copy(most, most, semaphore).wait()

    def node(local):
        depth = local.bit_length() - 1
        return (groups + group) * (1 << depth) + (local - (1 << depth))

    def lift_of(local):
        return leaf_tables[local - leaves, 0] if local >= leaves else lifts[node(local) - 4]

    def couple_of(local):
        return leaf_tables[local - leaves, 1] if local >= leaves else couples[node(local) - 2]

    def spread_of(local):
        return leaf_tables[local - leaves, 2] if local >= leaves else spreads[node(local) - 4]

    def first(chunk):
        wait_all(arrived.at[chunk], in_recv.at[chunk])
        wait_own(arrived.at[chunk], local_sem.at[0, chunk])
        up_sent[chunk] = row_dot(gather, arrived[chunk]).T.astype(jnp.bfloat16)
        seats(
            lambda other: tree_copy(
                up_sent.at[chunk, seat_rows(other)], up_got.at[chunk, seat], chunk, 0, (group, other)
            ).start()
        )
        up_got[chunk, seat] = up_sent[chunk, seat_rows(seat), :]

    def second(chunk):
        wait_up(chunk, tree_recv.at[0, chunk])
        skeletons = {leaves + index: up_got[chunk, index] for index in range(leaves)}
        for local in range(2 * leaves - 1, 1, -1):
            cross[chunk, local ^ 1] = times(couple_of(local), skeletons[local])
            if local % 2 == 0:
                skeletons[local // 2] = (
                    times(lift_of(local), skeletons[local])
                    + times(lift_of(local + 1), skeletons[local + 1])
                ).astype(jnp.bfloat16)
        top[chunk, groups + group] = skeletons[1]

        def body(shift, carry):
            tree_copy(
                top.at[chunk, groups + group],
                top.at[chunk, groups + group],
                chunk,
                1,
                (lax.rem(group + shift, groups), seat),
            ).start()
            return carry

        lax.fori_loop(1, groups, body, 0)

    def third(chunk):
        wait_top(chunk, tree_recv.at[1, chunk])
        for index in range(groups - 1, 1, -1):
            top[chunk, index] = (
                times(lifts[2 * index - 4], top[chunk, 2 * index])
                + times(lifts[2 * index - 3], top[chunk, 2 * index + 1])
            ).astype(jnp.bfloat16)
        incoming = None
        for height in range(groups.bit_length() - 2, -1, -1):
            mine = lax.div(groups + group, 1 << height)
            other = mine + 1 - 2 * lax.rem(mine, 2)
            crossed = times(couples[other - 2], top[chunk, other])
            if incoming is not None:
                crossed = crossed + fine_times(spreads[mine - 4], incoming)
            incoming = crossed
        passed = {1: incoming}
        for local in range(2, 2 * leaves):
            passed[local] = (
                fine_times(spread_of(local), passed[local // 2]) + cross[chunk, local]
            )
        for index in range(leaves):
            down_sent[chunk, index] = passed[leaves + index].astype(jnp.bfloat16)
        seats(
            lambda other: tree_copy(
                down_sent.at[chunk, other],
                down_got.at[chunk, seat_rows(seat)],
                chunk,
                2,
                (group, other),
            ).start()
        )
        down_got[chunk, seat_rows(seat), :] = down_sent[chunk, seat]

    def finish(chunk):
        wait_down(chunk, tree_recv.at[2, chunk])
        incoming = down_got[chunk].astype(jnp.float32).T.astype(jnp.bfloat16)

        def rows_done(index, carry):
            rows = pl.ds(pl.multiple_of(index * part, part), part)
            value = row_dot(diag_poles[rows, :], arrived[chunk]) + row_dot(
                out_poles[rows, :], incoming
            )
            staged[chunk, rows, :] = value.astype(jnp.bfloat16)
            return carry

        lax.fori_loop(0, width // part, rows_done, 0)
        send_out(chunk)

    stages = (first, second, third, finish)
    for tick in range(STRIDE * (chunks - 1) + len(stages)):
        for chunk in range(chunks):
            stage = tick - STRIDE * chunk
            if 0 <= stage < len(stages):
                stages[stage](chunk)
                if stage == 0 and chunk + AHEAD < chunks:
                    send_in(chunk + AHEAD)

    pltpu.make_async_copy(few, few, table_send.at[0]).wait()
    for chunk in range(chunks):
        wait_all(arrived.at[chunk], in_send.at[chunk])
        wait_up(chunk, tree_send.at[0, chunk])
        wait_top(chunk, tree_send.at[1, chunk])
        wait_down(chunk, tree_send.at[2, chunk])
        wait_all(staged.at[chunk], out_send.at[chunk])
        wait_all(staged.at[chunk], out_recv.at[chunk])
        wait_own(staged.at[chunk], local_sem.at[1, chunk])


def fused(
    basis_slab,
    live_counts,
    pole_order,
    leaf_diag,
    leaf_in,
    leaf_out,
    leaf_lift,
    leaf_couple,
    leaf_spread,
    inner_lift,
    inner_couple,
    inner_spread,
):
    groups = lax.axis_size("grp")
    leaves = lax.axis_size("leaf")
    devices = groups * leaves
    levels = devices.bit_length() - 1
    width, slab_rows = basis_slab.shape
    rank = leaf_in.shape[1]
    cols = slab_rows // CHUNKS
    vmem = pl.BlockSpec(memory_space=pltpu.VMEM)
    anywhere = pl.BlockSpec(memory_space=pl.ANY)
    half = jnp.bfloat16
    return pl.pallas_call(
        functools.partial(fused_kernel, groups, leaves),
        out_shape=jax.ShapeDtypeStruct((width, slab_rows), half),
        in_specs=[anywhere] + [vmem] * 2 + [anywhere] * 9,
        out_specs=anywhere,
        scratch_shapes=[
            pltpu.VMEM((CHUNKS, width, cols), half),
            pltpu.VMEM((CHUNKS, width, cols), half),
            pltpu.VMEM((width, width), half),
            pltpu.VMEM((width, rank), half),
            pltpu.VMEM((width, rank), half),
            pltpu.VMEM(inner_lift.shape, half),
            pltpu.VMEM(inner_couple.shape, half),
            pltpu.VMEM(inner_spread.shape, half),
            pltpu.VMEM((leaves, 3, rank, rank), half),
            pltpu.VMEM((width, width), half),
            pltpu.VMEM((width, width), half),
            pltpu.VMEM((width, rank), jnp.float32),
            pltpu.VMEM((width, rank), half),
            pltpu.VMEM((CHUNKS, cols, rank), half),
            pltpu.VMEM((CHUNKS, leaves, cols // leaves, rank), half),
            pltpu.VMEM((CHUNKS, 2 * groups, cols // leaves, rank), half),
            pltpu.VMEM((CHUNKS, 2 * leaves, cols // leaves, rank), jnp.float32),
            pltpu.VMEM((CHUNKS, leaves, cols // leaves, rank), half),
            pltpu.VMEM((CHUNKS, cols, rank), half),
            pltpu.SemaphoreType.DMA((CHUNKS,)),
            pltpu.SemaphoreType.DMA((CHUNKS,)),
            pltpu.SemaphoreType.DMA((CHUNKS,)),
            pltpu.SemaphoreType.DMA((CHUNKS,)),
            pltpu.SemaphoreType.DMA((3, CHUNKS)),
            pltpu.SemaphoreType.DMA((3, CHUNKS)),
            pltpu.SemaphoreType.DMA((2, CHUNKS)),
            pltpu.SemaphoreType.DMA((9,)),
            pltpu.SemaphoreType.DMA((1,)),
            pltpu.SemaphoreType.DMA((1,)),
        ],
        compiler_params=pltpu.CompilerParams(
            collective_id=0, has_side_effects=True, vmem_limit_bytes=56 * 1024 * 1024
        ),
    )(
        basis_slab,
        live_counts.reshape(1, 1),
        pole_order,
        leaf_diag,
        leaf_in,
        leaf_out,
        leaf_lift,
        leaf_couple,
        leaf_spread,
        inner_lift,
        inner_couple,
        inner_spread,
    )


def from_partner(block, axis, apart):
    count = lax.axis_size(axis)
    route = []
    for low in range(count):
        high = low | 1 << apart
        if high != low and high < count:
            route += [(low, high), (high, low)]
    return lax.ppermute(block, axis, route)


def transform(matrix, stacked):
    return jnp.dot(matrix.astype(jnp.float32), stacked, precision=lax.Precision.HIGHEST)


def local(
    basis_slab,
    live_counts,
    pole_order,
    leaf_diag,
    leaf_in,
    leaf_out,
    leaf_lift,
    leaf_couple,
    leaf_spread,
    inner_lift,
    inner_couple,
    inner_spread,
):
    groups = lax.axis_size("grp")
    leaves = lax.axis_size("leaf")
    devices = groups * leaves
    leaf_width = basis_slab.shape[0]
    slab_rows = basis_slab.shape[1]
    block_rows = leaf_width // devices
    levels = devices.bit_length() - 1
    leaf_bits = leaves.bit_length() - 1
    position = lax.axis_index("grp") * leaves + lax.axis_index("leaf")

    def redistribute(columns):
        arrived = lax.all_to_all(
            columns.reshape(devices, block_rows, slab_rows),
            ("grp", "leaf"),
            split_axis=0,
            concat_axis=0,
            tiled=True,
        )
        return arrived.reshape(leaf_width, slab_rows)

    def node_matrix(height, leaf_table, inner_table, offset):
        if height == 0:
            return leaf_table[0]
        own_node = jnp.right_shift(devices + position, height)
        return lax.dynamic_index_in_dim(inner_table, own_node - offset, 0, keepdims=False)

    leaf_rows = redistribute(basis_slab)
    slot_order = pole_order[0]
    live_count = live_counts[0]
    slots = jnp.take(leaf_rows, slot_order, axis=0)
    live_mask = jnp.arange(leaf_width, dtype=jnp.int32) < live_count
    masked = jnp.where(live_mask[:, None], slots, jnp.zeros_like(slots))
    skeleton = jnp.einsum("mk,mc->kc", leaf_in, masked, preferred_element_type=jnp.float32)
    crosses = []
    for height in range(leaf_bits):
        lifted = transform(node_matrix(height, leaf_lift, inner_lift, 4), skeleton)
        coupled = transform(node_matrix(height, leaf_couple, inner_couple, 2), skeleton)
        other_lift, other_cross = from_partner((lifted, coupled), "leaf", height)
        crosses.append(other_cross)
        skeleton = lifted + other_lift
    group_bits = groups.bit_length() - 1
    for height in range(leaf_bits, levels - 1):
        lifted = transform(node_matrix(height, leaf_lift, inner_lift, 4), skeleton)
        coupled = transform(node_matrix(height, leaf_couple, inner_couple, 2), skeleton)
        other_lift, other_cross = (
            from_partner(lifted.astype(jnp.bfloat16), "grp", height - leaf_bits).astype(
                lifted.dtype
            ),
            from_partner(coupled.astype(jnp.bfloat16), "grp", height - leaf_bits).astype(
                coupled.dtype
            ),
        )
        crosses.append(other_cross)
        skeleton = lifted + other_lift
    coupled = transform(node_matrix(levels - 1, leaf_couple, inner_couple, 2), skeleton)
    crosses.append(
        from_partner(coupled.astype(jnp.bfloat16), "grp", group_bits - 1).astype(coupled.dtype)
    )
    incoming = crosses[levels - 1]
    for height in range(levels - 2, -1, -1):
        incoming = (
            transform(node_matrix(height, leaf_spread, inner_spread, 4), incoming) + crosses[height]
        )
    incoming_b = incoming.astype(jnp.bfloat16)
    tile_rows = leaf_width // 8
    tile_count = live_count // tile_rows

    def one_tile(tile_index, merged_rows):
        row_start = tile_index * tile_rows
        diag_rows = lax.dynamic_slice_in_dim(leaf_diag, row_start, tile_rows, 0)
        out_rows = lax.dynamic_slice_in_dim(leaf_out, row_start, tile_rows, 0)
        value = jnp.dot(diag_rows, masked, preferred_element_type=jnp.float32) + jnp.dot(
            out_rows, incoming_b, preferred_element_type=jnp.float32
        )
        return lax.dynamic_update_slice_in_dim(merged_rows, value, row_start, 0)

    merged_rows = lax.fori_loop(
        0, tile_count, one_tile, jnp.zeros((leaf_width, slab_rows), jnp.float32)
    )
    updated = jnp.where(live_mask[:, None], merged_rows, slots.astype(jnp.float32)).astype(
        jnp.bfloat16
    )
    inverse = (
        jnp.zeros((leaf_width,), jnp.int32)
        .at[slot_order]
        .set(jnp.arange(leaf_width, dtype=jnp.int32))
    )
    restored = jnp.take(updated, inverse, axis=0)
    return redistribute(restored)


def solution(mesh):
    placed = (
        P(("grp", "leaf"), None),
        P(("grp", "leaf")),
        P(("grp", "leaf"), None),
        P(("grp", "leaf"), None),
        P(("grp", "leaf"), None),
        P(("grp", "leaf"), None),
        P(("grp", "leaf"), None, None),
        P(("grp", "leaf"), None, None),
        P(("grp", "leaf"), None, None),
        P(),
        P(),
        P(),
    )

    def step(basis_slab, *rest):
        devices = mesh.shape["grp"] * mesh.shape["leaf"]
        block_rows = basis_slab.shape[0] // devices
        whole_tiles = block_rows % 16 == 0 and basis_slab.shape[1] % (128 * CHUNKS) == 0 and basis_slab.shape[1] % (16 * CHUNKS * mesh.shape["leaf"]) == 0
        return (fused if whole_tiles else local)(basis_slab, *rest)

    return jax.shard_map(
        step, mesh=mesh, in_specs=placed, out_specs=P(("grp", "leaf"), None), check_vma=False
    )
```

```python
import functools

import jax
import jax.numpy as jnp
from jax import lax
from jax.experimental import pallas as pl
from jax.experimental.pallas import tpu as pltpu
from jax.sharding import PartitionSpec as P

MESH = pl.DeviceIdType.MESH
CHUNKS = 4
AHEAD = 2
STRIDE = 1


def row_dot(a, b):
    return jnp.dot(a, b, preferred_element_type=jnp.float32)


def times(matrix, rows):
    return lax.dot_general(
        rows, matrix, (((1,), (1,)), ((), ())), preferred_element_type=jnp.float32
    )


def fine_times(matrix, rows):
    high = rows.astype(jnp.bfloat16)
    low = (rows - high.astype(jnp.float32)).astype(jnp.bfloat16)
    return times(matrix, high) + times(matrix, low)


def fused_kernel(
    groups,
    leaves,
    slab,
    live,
    order,
    diag,
    gen_in,
    gen_out,
    leaf_lift,
    leaf_couple,
    leaf_spread,
    inner_lift,
    inner_couple,
    inner_spread,
    out,
    arrived,
    staged,
    diag_here,
    in_here,
    out_here,
    lifts,
    couples,
    spreads,
    leaf_tables,
    select,
    diag_poles,
    in_poles,
    out_poles,
    up_sent,
    up_got,
    top,
    cross,
    down_sent,
    down_got,
    in_send,
    in_recv,
    out_send,
    out_recv,
    tree_send,
    tree_recv,
    local_sem,
    load_sem,
    table_send,
    table_recv,
):
    devices = groups * leaves
    chunks, width, cols = arrived.shape
    block = width // devices
    part_cols = cols // leaves
    group = lax.axis_index("grp")
    seat = lax.axis_index("leaf")
    me = group * leaves + seat

    def place(device):
        return (lax.div(device, leaves), lax.rem(device, leaves))

    def node(height):
        return lax.div(devices + me, 1 << height)

    def sibling(index):
        return index + 1 - 2 * lax.rem(index, 2)

    def seats(step):
        def body(shift, carry):
            step(lax.rem(seat + shift, leaves))
            return carry

        lax.fori_loop(1, leaves, body, 0)

    def others(step):
        def body(shift, carry):
            step(lax.rem(me + shift, devices))
            return carry

        lax.fori_loop(1, devices, body, 0)

    def rows_of(device):
        return pl.ds(pl.multiple_of(device * block, block), block)

    def cols_of(chunk):
        return pl.ds(chunk * cols, cols)

    barrier = pltpu.get_barrier_semaphore()
    others(
        lambda device: pl.semaphore_signal(
            barrier, inc=1, device_id=place(device), device_id_type=MESH
        )
    )
    pl.semaphore_wait(barrier, devices - 1)

    def send_in(chunk):
        others(
            lambda device: pltpu.make_async_remote_copy(
                src_ref=slab.at[rows_of(device), cols_of(chunk)],
                dst_ref=arrived.at[chunk, rows_of(me)],
                send_sem=in_send.at[chunk],
                recv_sem=in_recv.at[chunk],
                device_id=place(device),
                device_id_type=MESH,
            ).start()
        )
        pltpu.make_async_copy(
            slab.at[rows_of(me), cols_of(chunk)],
            arrived.at[chunk, rows_of(me)],
            local_sem.at[0, chunk],
        ).start()

    def send_out(chunk):
        others(
            lambda device: pltpu.make_async_remote_copy(
                src_ref=staged.at[chunk, rows_of(device)],
                dst_ref=out.at[rows_of(me), cols_of(chunk)],
                send_sem=out_send.at[chunk],
                recv_sem=out_recv.at[chunk],
                device_id=place(device),
                device_id_type=MESH,
            ).start()
        )
        pltpu.make_async_copy(
            staged.at[chunk, rows_of(me)],
            out.at[rows_of(me), cols_of(chunk)],
            local_sem.at[1, chunk],
        ).start()

    def wait_all(buffer, semaphore):
        most = buffer.at[pl.ds(0, width - block)]
        pltpu.make_async_copy(most, most, semaphore).wait()

    def wait_own(buffer, semaphore):
        part = buffer.at[pl.ds(0, block)]
        pltpu.make_async_copy(part, part, semaphore).wait()

    def tree_copy(source, target, chunk, stage, device):
        return pltpu.make_async_remote_copy(
            src_ref=source,
            dst_ref=target,
            send_sem=tree_send.at[stage, chunk],
            recv_sem=tree_recv.at[stage, chunk],
            device_id=device,
            device_id_type=MESH,
        )

    own_tables = (leaf_lift, leaf_couple, leaf_spread)
    for index, table in enumerate(own_tables):
        seats(
            lambda other: pltpu.make_async_remote_copy(
                src_ref=table.at[0],
                dst_ref=leaf_tables.at[seat, index],
                send_sem=table_send.at[0],
                recv_sem=table_recv.at[0],
                device_id=(group, other),
                device_id_type=MESH,
            ).start()
        )

    for chunk in range(min(AHEAD, chunks)):
        send_in(chunk)

    pairs = [(diag, diag_here), (gen_in, in_here), (gen_out, out_here)]
    pairs += [(inner_lift, lifts), (inner_couple, couples), (inner_spread, spreads)]
    pairs += [(table.at[0], leaf_tables.at[seat, index]) for index, table in enumerate(own_tables)]
    loads = [
        pltpu.make_async_copy(source, target, load_sem.at[index])
        for index, (source, target) in enumerate(pairs)
    ]
    for load in loads:
        load.start()

    slot = lax.broadcasted_iota(jnp.int32, (1, width), 1)
    key = jnp.where(slot < live[...], order[...], -1)
    part = min(256, width)
    for start in range(0, width, part):
        pole = lax.broadcasted_iota(jnp.int32, (part, width), 0) + start
        select[start : start + part, :] = jnp.where(pole == key, 1.0, 0.0).astype(jnp.bfloat16)

    for load in loads:
        load.wait()

    def fold(index, carry):
        start = pl.multiple_of(index * part, part)
        rows = pl.ds(start, part)
        chosen = select[rows, :]
        half = row_dot(chosen, diag_here[...]).astype(jnp.bfloat16)
        full = lax.dot_general(
            half, select[...], (((1,), (1,)), ((), ())), preferred_element_type=jnp.float32
        )
        alive = jnp.sum(chosen.astype(jnp.float32), axis=1, keepdims=True)
        pole = lax.broadcasted_iota(jnp.int32, (part, width), 0) + start
        same = jnp.where(pole == lax.broadcasted_iota(jnp.int32, (part, width), 1), 1.0, 0.0)
        diag_poles[rows, :] = (full + (1.0 - alive) * same).astype(jnp.bfloat16)
        out_poles[rows, :] = row_dot(chosen, out_here[...]).astype(jnp.bfloat16)
        in_poles[rows, :] = row_dot(chosen, in_here[...])
        return carry

    lax.fori_loop(0, width // part, fold, 0)
    gather = in_poles[...].T.astype(jnp.bfloat16)

    few = leaf_tables.at[pl.ds(0, leaves - 1)]
    pltpu.make_async_copy(few, few, table_recv.at[0]).wait()

    def seat_rows(other):
        return pl.ds(pl.multiple_of(other * part_cols, part_cols), part_cols)

    def wait_up(chunk, semaphore):
        most = up_got.at[chunk, pl.ds(0, leaves - 1)]
        pltpu.make_async_copy(most, most, semaphore).wait()

    def wait_top(chunk, semaphore):
        most = top.at[chunk, pl.ds(0, groups - 1)]
        pltpu.make_async_copy(most, most, semaphore).wait()

    def wait_down(chunk, semaphore):
        most = down_got.at[chunk, pl.ds(0, cols - part_cols)]
        pltpu.make_async_copy(most, most, semaphore).wait()

    def node(local):
        depth = local.bit_length() - 1
        return (groups + group) * (1 << depth) + (local - (1 << depth))

    def lift_of(local):
        return leaf_tables[local - leaves, 0] if local >= leaves else lifts[node(local) - 4]

    def couple_of(local):
        return leaf_tables[local - leaves, 1] if local >= leaves else couples[node(local) - 2]

    def spread_of(local):
        return leaf_tables[local - leaves, 2] if local >= leaves else spreads[node(local) - 4]

    def first(chunk):
        wait_all(arrived.at[chunk], in_recv.at[chunk])
        wait_own(arrived.at[chunk], local_sem.at[0, chunk])
        up_sent[chunk] = row_dot(gather, arrived[chunk]).T.astype(jnp.bfloat16)
        seats(
            lambda other: tree_copy(
                up_sent.at[chunk, seat_rows(other)], up_got.at[chunk, seat], chunk, 0, (group, other)
            ).start()
        )
        up_got[chunk, seat] = up_sent[chunk, seat_rows(seat), :]

    def second(chunk):
        wait_up(chunk, tree_recv.at[0, chunk])
        skeletons = {leaves + index: up_got[chunk, index] for index in range(leaves)}
        for local in range(2 * leaves - 1, 1, -1):
            cross[chunk, local ^ 1] = times(couple_of(local), skeletons[local])
            if local % 2 == 0:
                skeletons[local // 2] = (
                    times(lift_of(local), skeletons[local])
                    + times(lift_of(local + 1), skeletons[local + 1])
                ).astype(jnp.bfloat16)
        top[chunk, groups + group] = skeletons[1]

        def body(shift, carry):
            tree_copy(
                top.at[chunk, groups + group],
                top.at[chunk, groups + group],
                chunk,
                1,
                (lax.rem(group + shift, groups), seat),
            ).start()
            return carry

        lax.fori_loop(1, groups, body, 0)

    def third(chunk):
        wait_top(chunk, tree_recv.at[1, chunk])
        for index in range(groups - 1, 1, -1):
            top[chunk, index] = (
                times(lifts[2 * index - 4], top[chunk, 2 * index])
                + times(lifts[2 * index - 3], top[chunk, 2 * index + 1])
            ).astype(jnp.bfloat16)
        incoming = None
        for height in range(groups.bit_length() - 2, -1, -1):
            mine = lax.div(groups + group, 1 << height)
            other = mine + 1 - 2 * lax.rem(mine, 2)
            crossed = times(couples[other - 2], top[chunk, other])
            if incoming is not None:
                crossed = crossed + fine_times(spreads[mine - 4], incoming)
            incoming = crossed
        passed = {1: incoming}
        for local in range(2, 2 * leaves):
            passed[local] = (
                fine_times(spread_of(local), passed[local // 2]) + cross[chunk, local]
            )
        for index in range(leaves):
            down_sent[chunk, index] = passed[leaves + index].astype(jnp.bfloat16)
        seats(
            lambda other: tree_copy(
                down_sent.at[chunk, other],
                down_got.at[chunk, seat_rows(seat)],
                chunk,
                2,
                (group, other),
            ).start()
        )
        down_got[chunk, seat_rows(seat), :] = down_sent[chunk, seat]

    def finish(chunk):
        wait_down(chunk, tree_recv.at[2, chunk])
        incoming = down_got[chunk].astype(jnp.float32).T.astype(jnp.bfloat16)

        def rows_done(index, carry):
            rows = pl.ds(pl.multiple_of(index * part, part), part)
            value = row_dot(diag_poles[rows, :], arrived[chunk]) + row_dot(
                out_poles[rows, :], incoming
            )
            staged[chunk, rows, :] = value.astype(jnp.bfloat16)
            return carry

        lax.fori_loop(0, width // part, rows_done, 0)
        send_out(chunk)

    stages = (first, second, third, finish)
    for tick in range(STRIDE * (chunks - 1) + len(stages)):
        for chunk in range(chunks):
            stage = tick - STRIDE * chunk
            if 0 <= stage < len(stages):
                stages[stage](chunk)
                if stage == 1 and chunk + AHEAD < chunks:
                    send_in(chunk + AHEAD)

    pltpu.make_async_copy(few, few, table_send.at[0]).wait()
    for chunk in range(chunks):
        wait_all(arrived.at[chunk], in_send.at[chunk])
        wait_up(chunk, tree_send.at[0, chunk])
        wait_top(chunk, tree_send.at[1, chunk])
        wait_down(chunk, tree_send.at[2, chunk])
        wait_all(staged.at[chunk], out_send.at[chunk])
        wait_all(staged.at[chunk], out_recv.at[chunk])
        wait_own(staged.at[chunk], local_sem.at[1, chunk])


def fused(
    basis_slab,
    live_counts,
    pole_order,
    leaf_diag,
    leaf_in,
    leaf_out,
    leaf_lift,
    leaf_couple,
    leaf_spread,
    inner_lift,
    inner_couple,
    inner_spread,
):
    groups = lax.axis_size("grp")
    leaves = lax.axis_size("leaf")
    devices = groups * leaves
    levels = devices.bit_length() - 1
    width, slab_rows = basis_slab.shape
    rank = leaf_in.shape[1]
    cols = slab_rows // CHUNKS
    vmem = pl.BlockSpec(memory_space=pltpu.VMEM)
    anywhere = pl.BlockSpec(memory_space=pl.ANY)
    half = jnp.bfloat16
    return pl.pallas_call(
        functools.partial(fused_kernel, groups, leaves),
        out_shape=jax.ShapeDtypeStruct((width, slab_rows), half),
        in_specs=[anywhere] + [vmem] * 2 + [anywhere] * 9,
        out_specs=anywhere,
        scratch_shapes=[
            pltpu.VMEM((CHUNKS, width, cols), half),
            pltpu.VMEM((CHUNKS, width, cols), half),
            pltpu.VMEM((width, width), half),
            pltpu.VMEM((width, rank), half),
            pltpu.VMEM((width, rank), half),
            pltpu.VMEM(inner_lift.shape, half),
            pltpu.VMEM(inner_couple.shape, half),
            pltpu.VMEM(inner_spread.shape, half),
            pltpu.VMEM((leaves, 3, rank, rank), half),
            pltpu.VMEM((width, width), half),
            pltpu.VMEM((width, width), half),
            pltpu.VMEM((width, rank), jnp.float32),
            pltpu.VMEM((width, rank), half),
            pltpu.VMEM((CHUNKS, cols, rank), half),
            pltpu.VMEM((CHUNKS, leaves, cols // leaves, rank), half),
            pltpu.VMEM((CHUNKS, 2 * groups, cols // leaves, rank), half),
            pltpu.VMEM((CHUNKS, 2 * leaves, cols // leaves, rank), jnp.float32),
            pltpu.VMEM((CHUNKS, leaves, cols // leaves, rank), half),
            pltpu.VMEM((CHUNKS, cols, rank), half),
            pltpu.SemaphoreType.DMA((CHUNKS,)),
            pltpu.SemaphoreType.DMA((CHUNKS,)),
            pltpu.SemaphoreType.DMA((CHUNKS,)),
            pltpu.SemaphoreType.DMA((CHUNKS,)),
            pltpu.SemaphoreType.DMA((3, CHUNKS)),
            pltpu.SemaphoreType.DMA((3, CHUNKS)),
            pltpu.SemaphoreType.DMA((2, CHUNKS)),
            pltpu.SemaphoreType.DMA((9,)),
            pltpu.SemaphoreType.DMA((1,)),
            pltpu.SemaphoreType.DMA((1,)),
        ],
        compiler_params=pltpu.CompilerParams(
            collective_id=0, has_side_effects=True, vmem_limit_bytes=56 * 1024 * 1024
        ),
    )(
        basis_slab,
        live_counts.reshape(1, 1),
        pole_order,
        leaf_diag,
        leaf_in,
        leaf_out,
        leaf_lift,
        leaf_couple,
        leaf_spread,
        inner_lift,
        inner_couple,
        inner_spread,
    )


def from_partner(block, axis, apart):
    count = lax.axis_size(axis)
    route = []
    for low in range(count):
        high = low | 1 << apart
        if high != low and high < count:
            route += [(low, high), (high, low)]
    return lax.ppermute(block, axis, route)


def transform(matrix, stacked):
    return jnp.dot(matrix.astype(jnp.float32), stacked, precision=lax.Precision.HIGHEST)


def local(
    basis_slab,
    live_counts,
    pole_order,
    leaf_diag,
    leaf_in,
    leaf_out,
    leaf_lift,
    leaf_couple,
    leaf_spread,
    inner_lift,
    inner_couple,
    inner_spread,
):
    groups = lax.axis_size("grp")
    leaves = lax.axis_size("leaf")
    devices = groups * leaves
    leaf_width = basis_slab.shape[0]
    slab_rows = basis_slab.shape[1]
    block_rows = leaf_width // devices
    levels = devices.bit_length() - 1
    leaf_bits = leaves.bit_length() - 1
    position = lax.axis_index("grp") * leaves + lax.axis_index("leaf")

    def redistribute(columns):
        arrived = lax.all_to_all(
            columns.reshape(devices, block_rows, slab_rows),
            ("grp", "leaf"),
            split_axis=0,
            concat_axis=0,
            tiled=True,
        )
        return arrived.reshape(leaf_width, slab_rows)

    def node_matrix(height, leaf_table, inner_table, offset):
        if height == 0:
            return leaf_table[0]
        own_node = jnp.right_shift(devices + position, height)
        return lax.dynamic_index_in_dim(inner_table, own_node - offset, 0, keepdims=False)

    leaf_rows = redistribute(basis_slab)
    slot_order = pole_order[0]
    live_count = live_counts[0]
    slots = jnp.take(leaf_rows, slot_order, axis=0)
    live_mask = jnp.arange(leaf_width, dtype=jnp.int32) < live_count
    masked = jnp.where(live_mask[:, None], slots, jnp.zeros_like(slots))
    skeleton = jnp.einsum("mk,mc->kc", leaf_in, masked, preferred_element_type=jnp.float32)
    crosses = []
    for height in range(leaf_bits):
        lifted = transform(node_matrix(height, leaf_lift, inner_lift, 4), skeleton)
        coupled = transform(node_matrix(height, leaf_couple, inner_couple, 2), skeleton)
        other_lift, other_cross = from_partner((lifted, coupled), "leaf", height)
        crosses.append(other_cross)
        skeleton = lifted + other_lift
    group_bits = groups.bit_length() - 1
    for height in range(leaf_bits, levels - 1):
        lifted = transform(node_matrix(height, leaf_lift, inner_lift, 4), skeleton)
        coupled = transform(node_matrix(height, leaf_couple, inner_couple, 2), skeleton)
        other_lift, other_cross = (
            from_partner(lifted.astype(jnp.bfloat16), "grp", height - leaf_bits).astype(
                lifted.dtype
            ),
            from_partner(coupled.astype(jnp.bfloat16), "grp", height - leaf_bits).astype(
                coupled.dtype
            ),
        )
        crosses.append(other_cross)
        skeleton = lifted + other_lift
    coupled = transform(node_matrix(levels - 1, leaf_couple, inner_couple, 2), skeleton)
    crosses.append(
        from_partner(coupled.astype(jnp.bfloat16), "grp", group_bits - 1).astype(coupled.dtype)
    )
    incoming = crosses[levels - 1]
    for height in range(levels - 2, -1, -1):
        incoming = (
            transform(node_matrix(height, leaf_spread, inner_spread, 4), incoming) + crosses[height]
        )
    incoming_b = incoming.astype(jnp.bfloat16)
    tile_rows = leaf_width // 8
    tile_count = live_count // tile_rows

    def one_tile(tile_index, merged_rows):
        row_start = tile_index * tile_rows
        diag_rows = lax.dynamic_slice_in_dim(leaf_diag, row_start, tile_rows, 0)
        out_rows = lax.dynamic_slice_in_dim(leaf_out, row_start, tile_rows, 0)
        value = jnp.dot(diag_rows, masked, preferred_element_type=jnp.float32) + jnp.dot(
            out_rows, incoming_b, preferred_element_type=jnp.float32
        )
        return lax.dynamic_update_slice_in_dim(merged_rows, value, row_start, 0)

    merged_rows = lax.fori_loop(
        0, tile_count, one_tile, jnp.zeros((leaf_width, slab_rows), jnp.float32)
    )
    updated = jnp.where(live_mask[:, None], merged_rows, slots.astype(jnp.float32)).astype(
        jnp.bfloat16
    )
    inverse = (
        jnp.zeros((leaf_width,), jnp.int32)
        .at[slot_order]
        .set(jnp.arange(leaf_width, dtype=jnp.int32))
    )
    restored = jnp.take(updated, inverse, axis=0)
    return redistribute(restored)


def solution(mesh):
    placed = (
        P(("grp", "leaf"), None),
        P(("grp", "leaf")),
        P(("grp", "leaf"), None),
        P(("grp", "leaf"), None),
        P(("grp", "leaf"), None),
        P(("grp", "leaf"), None),
        P(("grp", "leaf"), None, None),
        P(("grp", "leaf"), None, None),
        P(("grp", "leaf"), None, None),
        P(),
        P(),
        P(),
    )

    def step(basis_slab, *rest):
        devices = mesh.shape["grp"] * mesh.shape["leaf"]
        block_rows = basis_slab.shape[0] // devices
        whole_tiles = block_rows % 16 == 0 and basis_slab.shape[1] % (128 * CHUNKS) == 0 and basis_slab.shape[1] % (16 * CHUNKS * mesh.shape["leaf"]) == 0
        return (fused if whole_tiles else local)(basis_slab, *rest)

    return jax.shard_map(
        step, mesh=mesh, in_specs=placed, out_specs=P(("grp", "leaf"), None), check_vma=False
    )
```
